32 devices in a mesh: row: 4 (over z), col: 8 (over y, x, core).
Axes of the slice: x: 2, y: 2, z: 4, core: 2. Of those that a mesh axis runs over, the one named last changes fastest.
Arguments:
- features: bfloat16 [8, 1024, 256], P('col', 'row'), may hold values from -6 to 6
- weight: bfloat16 [256, 256], replicated, may hold values from -0.375 to 0.375
- cotangent: bfloat16 [8192, 256], P(('row', 'col')), may hold values from -6 to 6
- blk_vals: bfloat16 [4, 8, 192, 128, 128], P('row', 'col'), may hold values from -0.0546875 to 0.0546875
- blk_rows: int32 [4, 8, 192], P('row', 'col'), may hold values from 0 to 15
- blk_cols: int32 [4, 8, 192], P('row', 'col'), may hold values from 0 to 7
- blk_count: int32 [4, 8], P('row', 'col'), may hold values from 24 to 192, as said below
Outputs:
- activated: bfloat16 [8192, 256], P(('row', 'col'))
- grad_weight: float32 [256, 256], replicated
- grad_features: bfloat16 [8, 1024, 256], P('col', 'row')
The draws below stay inside these ranges and needn't reach their ends.
Inputs may be any that keep to these rules, and one draw needn't show every extreme that they name: Only the first blk_count slots of a panel pair are used; a pair whose row and column node ranges intersect uses all 192, every other pair at most 96.
All inputs are finite; a program needn't handle non-finite values.
Results may differ from the reference program's by a relative error of at most 0.0059.
Values may be sent and summed in bfloat16 or wider, within the bound.
A program may use at most 128 MiB of HBM per device.

```python
import jax
import jax.numpy as jnp
from jax import lax

F = 256
BLOCK = 128
ROWS_DEV = 256
NBLK = 192
NODES = 8192
PANEL_COLS = 1024
BLOCK_ROWS = 16
BLOCK_COLS = 8
N_ROW = 4
N_COL = 8


def layout_draw(key):
    base = jax.random.fold_in(key, 91)
    keys = jax.random.split(base, 6)
    shape = (N_ROW, N_COL, NBLK)
    panel_r = jnp.arange(N_ROW, dtype=jnp.int32)[:, None] + jnp.zeros((N_ROW, N_COL), jnp.int32)
    panel_c = jnp.arange(N_COL, dtype=jnp.int32)[None, :] + jnp.zeros((N_ROW, N_COL), jnp.int32)
    row_low = panel_r * BLOCK_ROWS
    row_high = row_low + BLOCK_ROWS
    col_low = panel_c * BLOCK_COLS
    col_high = col_low + BLOCK_COLS
    lower = jnp.maximum(row_low, col_low)
    upper = jnp.minimum(row_high, col_high)
    near = upper > lower
    span = jnp.maximum(upper - lower, 1)
    diagonal = lower[..., None] + jax.random.randint(keys[0], shape, 0, 1 << 20) % span[..., None]
    near_rows = jnp.clip(diagonal + jax.random.randint(keys[1], shape, -4, 5), row_low[..., None], row_high[..., None] - 1) - row_low[..., None]
    near_cols = jnp.clip(diagonal + jax.random.randint(keys[2], shape, -4, 5), col_low[..., None], col_high[..., None] - 1) - col_low[..., None]
    far_rows = jax.random.randint(keys[3], shape, 0, BLOCK_ROWS)
    far_cols = jax.random.randint(keys[4], shape, 0, BLOCK_COLS)
    rows = jnp.where(near[..., None], near_rows, far_rows).astype(jnp.int32)
    cols = jnp.where(near[..., None], near_cols, far_cols).astype(jnp.int32)
    far_counts = jax.random.randint(keys[5], (N_ROW, N_COL), NBLK // 8, NBLK // 2 + 1)
    counts = jnp.where(near, NBLK, far_counts).astype(jnp.int32)
    return (rows, cols, counts)


def draw_blk_rows(key, part):
    return layout_draw(key)[0]


def draw_blk_cols(key, part):
    return layout_draw(key)[1]


def draw_blk_count(key, part):
    return layout_draw(key)[2]


def steps_of(stream_key, extent, pieces, smallest, high):
    level, own = 1.0, jax.random.fold_in(stream_key, 6)
    for axis_at, shards_of in pieces:
        heights = jnp.exp(jax.random.uniform(jax.random.fold_in(own, axis_at), (shards_of,), jnp.float32, smallest / len(pieces), high / len(pieces)))
        level = level * jnp.repeat(heights, extent[axis_at] // shards_of).reshape([-1 if axis == axis_at else 1 for axis in range(len(extent))])
    return level


def normal_values(stream_key, extent, deviation, limit, shards=(), kind=jnp.bfloat16):
    factor_of = steps_of(stream_key, extent, shards, -0.22, 0.18) if shards else 1.0
    result = jax.random.normal(stream_key, extent, jnp.float32) * deviation * factor_of
    return jnp.minimum(jnp.maximum(result, -limit), limit).astype(kind)


def setup_inputs(seed: int = 0) -> dict:
    splits = jax.random.split(jax.random.key(seed), 8)
    return {
        "features": normal_values(splits[0], (N_COL, PANEL_COLS, F), 1.0, 6.0, ((0, 8), (1, 4))),
        "weight": normal_values(splits[1], (F, F), F ** -0.5, 0.375),
        "cotangent": normal_values(splits[2], (NODES, F), 1.0, 6.0, ((0, 32),)),
        "blk_vals": normal_values(splits[3], (N_ROW, N_COL, NBLK, BLOCK, BLOCK), (NBLK * BLOCK * BLOCK // ROWS_DEV) ** -0.5, 0.0546875, ((0, 4), (1, 8))),
        "blk_rows": draw_blk_rows(jax.random.fold_in(splits[7], 71), 0),
        "blk_cols": draw_blk_cols(jax.random.fold_in(splits[7], 71), 0),
        "blk_count": draw_blk_count(jax.random.fold_in(splits[7], 71), 0),
    }


def reference(features, weight, cotangent, blk_vals, blk_rows, blk_cols, blk_count):
    width = features.shape[-1]
    row_blocks = ROWS_DEV * N_COL // BLOCK
    col_blocks = ROWS_DEV * N_ROW // BLOCK
    slot_ids = jnp.arange(NBLK, dtype=jnp.int32)

    def forward_step(accum, device):
        panel_r = device // N_COL
        panel_c = device % N_COL
        values = blk_vals[panel_r, panel_c].astype(jnp.float32)
        live = (slot_ids < blk_count[panel_r, panel_c]).astype(jnp.float32)
        source = features[panel_c].reshape(col_blocks, BLOCK, width)
        picked = source[blk_cols[panel_r, panel_c]].astype(jnp.float32)
        product = jnp.einsum('bij,bjf->bif', values, picked) * live[:, None, None]
        partial_sum = jax.ops.segment_sum(product, blk_rows[panel_r, panel_c], num_segments=row_blocks)
        return accum.at[panel_r].add(partial_sum), None

    start_fwd = jnp.zeros((N_ROW, row_blocks, BLOCK, width), jnp.float32)
    devices = jnp.arange(N_ROW * N_COL, dtype=jnp.int32)
    total_fwd, unused = lax.scan(forward_step, start_fwd, devices)
    aggregated = total_fwd.reshape(NODES, width).astype(jnp.bfloat16)
    pre = jnp.dot(aggregated, weight, preferred_element_type=jnp.float32)
    sigma = jax.nn.sigmoid(pre)
    activated = (pre * sigma).astype(jnp.bfloat16)
    grad_pre = (cotangent.astype(jnp.float32) * sigma * (1.0 + pre * (1.0 - sigma))).astype(jnp.bfloat16)
    grad_weight = jnp.dot(aggregated.T, grad_pre, preferred_element_type=jnp.float32)
    grad_agg = jnp.dot(grad_pre, weight.T, preferred_element_type=jnp.float32).astype(jnp.bfloat16)
    grad_blocks = grad_agg.reshape(N_ROW, row_blocks, BLOCK, width)

    def backward_step(accum, device):
        panel_r = device // N_COL
        panel_c = device % N_COL
        values = blk_vals[panel_r, panel_c].astype(jnp.float32)
        live = (slot_ids < blk_count[panel_r, panel_c]).astype(jnp.float32)
        picked = grad_blocks[panel_r][blk_rows[panel_r, panel_c]].astype(jnp.float32)
        product = jnp.einsum('bji,bjf->bif', values, picked) * live[:, None, None]
        partial_sum = jax.ops.segment_sum(product, blk_cols[panel_r, panel_c], num_segments=col_blocks)
        return accum.at[panel_c].add(partial_sum), None

    start_bwd = jnp.zeros((N_COL, col_blocks, BLOCK, width), jnp.float32)
    total_bwd, unused_b = lax.scan(backward_step, start_bwd, devices)
    grad_features = total_bwd.reshape(N_COL, ROWS_DEV * N_ROW, width).astype(jnp.bfloat16)
    return (activated, grad_weight, grad_features)
```

```python
import functools

import jax
import jax.numpy as jnp
from jax import lax
from jax.experimental import pallas as pl
from jax.experimental.pallas import tpu as pltpu
from jax.sharding import PartitionSpec as P

MESH = pl.DeviceIdType.MESH
F32 = jnp.float32
BF16 = jnp.bfloat16
DENSE_LIMIT = 16 * 1024 * 1024


def block_terms(values, index, source, live_count, transpose):
    total_slots = values.shape[0]
    group = 64
    width = source.shape[-1]
    side = values.shape[-1]
    if transpose:
        form = "bji,bjf->bif"
    else:
        form = "bij,bjf->bif"

    def one_group(group_index, buffer):
        first = group_index * group
        block_vals = lax.dynamic_slice_in_dim(values, first, group, 0)
        block_ids = lax.dynamic_slice_in_dim(index, first, group, 0)
        picked = jnp.take(source, block_ids, axis=0)
        product = jnp.einsum(form, block_vals, picked, preferred_element_type=jnp.float32)
        alive = first + jnp.arange(group, dtype=jnp.int32) < live_count
        product = jnp.where(alive[:, None, None], product, 0.0)
        return lax.dynamic_update_slice_in_dim(buffer, product, first, 0)

    buffer = jnp.zeros((total_slots, side, width), jnp.float32)
    groups = total_slots // group
    return lax.fori_loop(0, groups, one_group, buffer)


def blockwise_device(features, weight, cotangent, blk_vals, blk_rows, blk_cols, blk_count):
    rows_here = cotangent.shape[0]
    width = cotangent.shape[1]
    side = blk_vals.shape[-1]
    row_blocks = rows_here * lax.axis_size("col") // side
    col_blocks = rows_here * lax.axis_size("row") // side
    values = blk_vals[0, 0]
    row_ids = blk_rows[0, 0]
    col_ids = blk_cols[0, 0]
    live_count = blk_count[0, 0]
    panel = lax.all_gather(features, "row", axis=1, tiled=True)
    source = panel.reshape(col_blocks, side, width)
    products = block_terms(values, col_ids, source, live_count, False)
    partial_rows = jax.ops.segment_sum(products, row_ids, num_segments=row_blocks)
    own_rows = lax.psum_scatter(
        partial_rows.reshape(row_blocks * side, width), "col", scatter_dimension=0, tiled=True
    )
    aggregated = own_rows.astype(jnp.bfloat16)
    pre = jnp.dot(aggregated, weight, preferred_element_type=jnp.float32)
    sigma = jax.nn.sigmoid(pre)
    activated = (pre * sigma).astype(jnp.bfloat16)
    grad_pre = (cotangent.astype(jnp.float32) * sigma * (1.0 + pre * (1.0 - sigma))).astype(
        jnp.bfloat16
    )
    local_weight = lax.dot_general(
        aggregated, grad_pre, (((0,), (0,)), ((), ())), preferred_element_type=jnp.float32
    )
    grad_weight = lax.psum(local_weight, ("row", "col"))
    grad_agg = lax.dot_general(
        grad_pre, weight, (((1,), (1,)), ((), ())), preferred_element_type=jnp.float32
    ).astype(jnp.bfloat16)
    grad_rows = lax.all_gather(grad_agg, "col", axis=0, tiled=True)
    grad_source = grad_rows.reshape(row_blocks, side, width)
    back_products = block_terms(values, row_ids, grad_source, live_count, True)
    partial_cols = jax.ops.segment_sum(back_products, col_ids, num_segments=col_blocks)
    own_cols = lax.psum_scatter(
        partial_cols.reshape(col_blocks * side, width), "row", scatter_dimension=0, tiled=True
    )
    grad_features = own_cols.astype(jnp.bfloat16).reshape(1, rows_here, width)
    return (activated, grad_weight, grad_features)


def densify_kernel(cb, rows_ref, cols_ref, count_ref, vals_ref, out_ref, acc):
    step = pl.program_id(0)
    chunk, side = vals_ref.shape[0], vals_ref.shape[1]
    cells = acc.shape[0]

    @pl.when(step == 0)
    def _():
        def zero(i, carry):
            acc[i] = jnp.zeros((side, side), F32)
            return carry

        lax.fori_loop(0, cells, zero, 0)

    first = step * chunk
    live = jnp.clip(count_ref[0] - first, 0, chunk)

    def add(i, carry):
        slot = first + i
        cell = rows_ref[slot] * cb + cols_ref[slot]
        acc[cell] = acc[cell] + vals_ref[i].astype(F32)
        return carry

    lax.fori_loop(0, live, add, 0)

    @pl.when(step == pl.num_programs(0) - 1)
    def _():
        def put(i, carry):
            for j in range(cb):
                out_ref[pl.ds(pl.multiple_of(i * side, side), side), j * side : (j + 1) * side] = acc[
                    i * cb + j
                ].astype(BF16)
            return carry

        lax.fori_loop(0, cells // cb, put, 0)


def densify(values, row_ids, col_ids, count, rb, cb):
    slots, side = values.shape[0], values.shape[1]
    chunk = 32
    return pl.pallas_call(
        functools.partial(densify_kernel, cb),
        out_shape=jax.ShapeDtypeStruct((rb * side, cb * side), BF16),
        grid_spec=pltpu.PrefetchScalarGridSpec(
            num_scalar_prefetch=3,
            grid=(slots // chunk,),
            in_specs=[pl.BlockSpec((chunk, side, side), lambda i, *_: (i, 0, 0))],
            out_specs=pl.BlockSpec((rb * side, cb * side), lambda i, *_: (0, 0)),
            scratch_shapes=[pltpu.VMEM((rb * cb, side, side), F32)],
        ),
        name="densify",
    )(row_ids, col_ids, count, values)


def layer_kernel(
    nr, nc,
    x_ref, w_ref, ct_ref, a_hbm, act_ref, gw_ref, gf_ref,
    a_ref, xs, pf, sib_out, sib_in, chip_out, chip_in, gbuf, qt, z_out, z_in,
    lw, gw_in, gw_own, gw_row, gw_all,
    a_sem, x_s, x_r, sib_s, sib_r, chip_s, chip_r, g_s, g_r, f_s, f_r, z_s, z_r,
    w1_s, w1_r, w2_s, w2_r, w3_s, w3_r,
):
    r = lax.axis_index("row")
    c = lax.axis_index("col")
    nq = nc // 2
    q = c // 2
    core = c % 2
    sib = 2 * q + (1 - core)
    rd, width = x_ref.shape
    wr = width // nc

    def remote(src, dst, s, t, where):
        return pltpu.make_async_remote_copy(
            src_ref=src, dst_ref=dst, send_sem=s, recv_sem=t, device_id=where, device_id_type=MESH
        )

    load_a = pltpu.make_async_copy(a_hbm, a_ref, a_sem)
    load_a.start()

    barrier = pltpu.get_barrier_semaphore()
    for j in range(1, nr):
        pl.semaphore_signal(barrier, inc=1, device_id={"row": (r + j) % nr}, device_id_type=MESH)
    for j in range(1, nc):
        pl.semaphore_signal(barrier, inc=1, device_id={"col": (c + j) % nc}, device_id_type=MESH)
    pl.semaphore_wait(barrier, nr + nc - 2)

    def rows(i):
        return pl.ds(pl.multiple_of(i * rd, rd), rd)

    x_copies = [
        remote(x_ref, xs.at[j - 1], x_s.at[j - 1], x_r.at[j - 1], {"row": (r + j) % nr})
        for j in range(1, nr)
    ]
    for copy in x_copies:
        copy.start()
    load_a.wait()

    def own_term(d, carry):
        pf[d] = jnp.dot(a_ref[rows(d), rows(r)], x_ref[...], preferred_element_type=F32)
        return carry

    lax.fori_loop(0, nc, own_term, 0)
    order = sorted(range(1, nr), key=lambda j: min(j, nr - j))
    for j in order[:-1]:
        x_copies[j - 1].wait_recv()

        def add_term(d, carry, j=j):
            pf[d] += jnp.dot(
                a_ref[rows(d), rows((r + nr - j) % nr)], xs[j - 1], preferred_element_type=F32
            )
            return carry

        lax.fori_loop(0, nc, add_term, 0)
    last = order[-1]
    x_copies[last - 1].wait_recv()

    def total(d):
        return pf[d] + jnp.dot(
            a_ref[rows(d), rows((r + nr - last) % nr)], xs[last - 1], preferred_element_type=F32
        )

    sib_copies = []
    for t in range(nq):
        chip = (q + t + 1) % nq
        sib_out[t] = total(2 * chip + (1 - core)).astype(BF16)
        copy = remote(sib_out.at[t], sib_in.at[t], sib_s.at[t], sib_r.at[t], {"col": sib})
        copy.start()
        sib_copies.append(copy)
    chip_copies = []
    for t in range(nq):
        d = 2 * ((q + t + 1) % nq) + core
        value = total(d)
        sib_copies[t].wait_recv()
        value = value + sib_in[t].astype(F32)
        if t < nq - 1:
            chip_out[t] = value.astype(BF16)
            copy = remote(chip_out.at[t], chip_in.at[t], chip_s.at[t], chip_r.at[t], {"col": d})
            copy.start()
            chip_copies.append(copy)
        else:
            pf[0] = value
    agg = pf[0]
    for t in range(nq - 1):
        chip_copies[t].wait_recv()
        agg = agg + chip_in[t].astype(F32)
    agg = agg.astype(BF16)

    pre = jnp.dot(agg, w_ref[...], preferred_element_type=F32)
    sigma = jax.nn.sigmoid(pre)
    act_ref[...] = (pre * sigma).astype(BF16)
    grad_pre = (ct_ref[...].astype(F32) * sigma * (1.0 + pre * (1.0 - sigma))).astype(BF16)
    gbuf[0, 0] = lax.dot_general(
        w_ref[...], grad_pre, (((1,), (1,)), ((), ())), preferred_element_type=F32
    ).astype(BF16)

    g_copies = [
        remote(gbuf.at[0, 0], gbuf.at[j, 0], g_s.at[j - 1], g_r.at[j - 1], {"col": 2 * ((q + j) % nq) + core})
        for j in range(1, nq)
    ]
    f_copies = [
        remote(gbuf.at[j, 0], gbuf.at[j, 1], f_s.at[j], f_r.at[j], {"col": sib}) for j in range(nq)
    ]
    for copy in g_copies:
        copy.start()
    f_copies[0].start()

    lw[...] = lax.dot_general(agg, grad_pre, (((0,), (0,)), ((), ())), preferred_element_type=F32)
    w1 = []
    for j in range(1, nc):
        d = (c + j) % nc
        copy = remote(
            lw.at[pl.ds(pl.multiple_of(d * wr, wr), wr), :], gw_in.at[j - 1],
            w1_s.at[j - 1], w1_r.at[j - 1], {"col": d},
        )
        copy.start()
        w1.append(copy)

    def a_rows(j, e):
        return rows(2 * ((q + nq - j) % nq) + (core if e == 0 else 1 - core))

    qt[...] = jnp.dot(gbuf[0, 0], a_ref[a_rows(0, 0), :], preferred_element_type=F32)
    for j in range(1, nq):
        f_copies[j - 1].wait_recv()
        qt[...] += jnp.dot(gbuf[j - 1, 1], a_ref[a_rows(j - 1, 1), :], preferred_element_type=F32)
        g_copies[j - 1].wait_recv()
        f_copies[j].start()
        qt[...] += jnp.dot(gbuf[j, 0], a_ref[a_rows(j, 0), :], preferred_element_type=F32)

    own_gw = lw[pl.ds(pl.multiple_of(c * wr, wr), wr), :]
    for copy in w1:
        copy.wait_recv()
    for j in range(1, nc):
        own_gw = own_gw + gw_in[j - 1]
    gw_own[...] = own_gw
    w2 = []
    for j in range(1, nr):
        copy = remote(gw_own, gw_row.at[j - 1], w2_s.at[j - 1], w2_r.at[j - 1], {"row": (r + j) % nr})
        copy.start()
        w2.append(copy)

    f_copies[nq - 1].wait_recv()
    z_copies = []
    for j in range(1, nr + 1):
        k = (r + j) % nr
        cols = rows(k)
        part = qt[:, cols] + jnp.dot(
            gbuf[nq - 1, 1], a_ref[a_rows(nq - 1, 1), cols], preferred_element_type=F32
        )
        if j < nr:
            z_out[j - 1] = part.astype(BF16)
            copy = remote(z_out.at[j - 1], z_in.at[j - 1], z_s.at[j - 1], z_r.at[j - 1], {"row": k})
            copy.start()
            z_copies.append(copy)
        else:
            pf[0] = part

    for copy in w2:
        copy.wait_recv()
    term = lambda i: jnp.where(
        i == r, own_gw, gw_row[jnp.maximum((r + nr - i) % nr, 1) - 1]
    )
    full = term(0)
    for i in range(1, nr):
        full = full + term(i)
    mine = pl.ds(pl.multiple_of(c * wr, wr), wr)
    gw_all[mine, :] = full
    w3 = []
    for j in range(1, nc):
        copy = remote(
            gw_all.at[mine, :], gw_all.at[mine, :], w3_s.at[j - 1], w3_r.at[j - 1], {"col": (c + j) % nc}
        )
        copy.start()
        w3.append(copy)

    grad = pf[0]
    for j in order:
        z_copies[j - 1].wait_recv()
        grad = grad + z_in[j - 1].astype(F32)
    gf_ref[...] = jnp.transpose(grad).astype(BF16)
    for copy in w3:
        copy.wait_recv()
    gw_ref[...] = gw_all[...]
    for copy in x_copies + sib_copies + chip_copies + g_copies + f_copies + w1 + w2 + z_copies + w3:
        copy.wait_send()


def dense_device(features, weight, cotangent, blk_vals, blk_rows, blk_cols, blk_count):
    nr, nc = lax.axis_size("row"), lax.axis_size("col")
    nq = nc // 2
    rd, width = cotangent.shape
    side = blk_vals.shape[-1]
    rb, cb = rd * nc // side, rd * nr // side
    panel = densify(blk_vals[0, 0], blk_rows[0, 0], blk_cols[0, 0], blk_count[0], rb, cb)
    vmem = pl.BlockSpec(memory_space=pltpu.VMEM)
    dma = pltpu.SemaphoreType.DMA
    wr = width // nc
    activated, grad_weight, grad_features = pl.pallas_call(
        functools.partial(layer_kernel, nr, nc),
        out_shape=(
            jax.ShapeDtypeStruct((rd, width), BF16),
            jax.ShapeDtypeStruct((width, width), F32),
            jax.ShapeDtypeStruct((rd, width), BF16),
        ),
        in_specs=[vmem, vmem, vmem, pl.BlockSpec(memory_space=pl.ANY)],
        out_specs=(vmem, vmem, vmem),
        scratch_shapes=[
            pltpu.VMEM((rd * nc, rd * nr), BF16),
            pltpu.VMEM((nr - 1, rd, width), BF16),
            pltpu.VMEM((nc, rd, width), F32),
            pltpu.VMEM((nq, rd, width), BF16),
            pltpu.VMEM((nq, rd, width), BF16),
            pltpu.VMEM((nq - 1, rd, width), BF16),
            pltpu.VMEM((nq - 1, rd, width), BF16),
            pltpu.VMEM((nq, 2, width, rd), BF16),
            pltpu.VMEM((width, rd * nr), F32),
            pltpu.VMEM((nr - 1, width, rd), BF16),
            pltpu.VMEM((nr - 1, width, rd), BF16),
            pltpu.VMEM((width, width), F32),
            pltpu.VMEM((nc - 1, wr, width), F32),
            pltpu.VMEM((wr, width), F32),
            pltpu.VMEM((nr - 1, wr, width), F32),
            pltpu.VMEM((width, width), F32),
            dma(()),
            dma((nr - 1,)), dma((nr - 1,)),
            dma((nq,)), dma((nq,)),
            dma((nq - 1,)), dma((nq - 1,)),
            dma((nq - 1,)), dma((nq - 1,)),
            dma((nq,)), dma((nq,)),
            dma((nr - 1,)), dma((nr - 1,)),
            dma((nc - 1,)), dma((nc - 1,)),
            dma((nr - 1,)), dma((nr - 1,)),
            dma((nc - 1,)), dma((nc - 1,)),
        ],
        compiler_params=pltpu.CompilerParams(collective_id=0, has_side_effects=True),
        name="layer",
    )(features[0], weight, cotangent, panel)
    return activated, grad_weight, grad_features[None]


def per_device(*arrays):
    blk_vals, cotangent = arrays[3], arrays[2]
    rd = cotangent.shape[0]
    panel_bytes = rd * lax.axis_size("col") * rd * lax.axis_size("row") * 4
    if panel_bytes <= DENSE_LIMIT:
        return dense_device(*arrays)
    return blockwise_device(*arrays)


def solution(mesh):
    return jax.shard_map(
        per_device,
        mesh=mesh,
        in_specs=(
            P("col", "row", None),
            P(),
            P(("row", "col"), None),
            P("row", "col", None, None, None),
            P("row", "col", None),
            P("row", "col", None),
            P("row", "col"),
        ),
        out_specs=(P(("row", "col"), None), P(), P("col", "row", None)),
        check_vma=False,
    )
```

```python
import functools

import jax
import jax.numpy as jnp
from jax import lax
from jax.experimental import pallas as pl
from jax.experimental.pallas import tpu as pltpu
from jax.sharding import PartitionSpec as P

MESH = pl.DeviceIdType.MESH
F32 = jnp.float32
BF16 = jnp.bfloat16
DENSE_LIMIT = 16 * 1024 * 1024


def block_terms(values, index, source, live_count, transpose):
    total_slots = values.shape[0]
    group = 64
    width = source.shape[-1]
    side = values.shape[-1]
    if transpose:
        form = "bji,bjf->bif"
    else:
        form = "bij,bjf->bif"

    def one_group(group_index, buffer):
        first = group_index * group
        block_vals = lax.dynamic_slice_in_dim(values, first, group, 0)
        block_ids = lax.dynamic_slice_in_dim(index, first, group, 0)
        picked = jnp.take(source, block_ids, axis=0)
        product = jnp.einsum(form, block_vals, picked, preferred_element_type=jnp.float32)
        alive = first + jnp.arange(group, dtype=jnp.int32) < live_count
        product = jnp.where(alive[:, None, None], product, 0.0)
        return lax.dynamic_update_slice_in_dim(buffer, product, first, 0)

    buffer = jnp.zeros((total_slots, side, width), jnp.float32)
    groups = total_slots // group
    return lax.fori_loop(0, groups, one_group, buffer)


def blockwise_device(features, weight, cotangent, blk_vals, blk_rows, blk_cols, blk_count):
    rows_here = cotangent.shape[0]
    width = cotangent.shape[1]
    side = blk_vals.shape[-1]
    row_blocks = rows_here * lax.axis_size("col") // side
    col_blocks = rows_here * lax.axis_size("row") // side
    values = blk_vals[0, 0]
    row_ids = blk_rows[0, 0]
    col_ids = blk_cols[0, 0]
    live_count = blk_count[0, 0]
    panel = lax.all_gather(features, "row", axis=1, tiled=True)
    source = panel.reshape(col_blocks, side, width)
    products = block_terms(values, col_ids, source, live_count, False)
    partial_rows = jax.ops.segment_sum(products, row_ids, num_segments=row_blocks)
    own_rows = lax.psum_scatter(
        partial_rows.reshape(row_blocks * side, width), "col", scatter_dimension=0, tiled=True
    )
    aggregated = own_rows.astype(jnp.bfloat16)
    pre = jnp.dot(aggregated, weight, preferred_element_type=jnp.float32)
    sigma = jax.nn.sigmoid(pre)
    activated = (pre * sigma).astype(jnp.bfloat16)
    grad_pre = (cotangent.astype(jnp.float32) * sigma * (1.0 + pre * (1.0 - sigma))).astype(
        jnp.bfloat16
    )
    local_weight = lax.dot_general(
        aggregated, grad_pre, (((0,), (0,)), ((), ())), preferred_element_type=jnp.float32
    )
    grad_weight = lax.psum(local_weight, ("row", "col"))
    grad_agg = lax.dot_general(
        grad_pre, weight, (((1,), (1,)), ((), ())), preferred_element_type=jnp.float32
    ).astype(jnp.bfloat16)
    grad_rows = lax.all_gather(grad_agg, "col", axis=0, tiled=True)
    grad_source = grad_rows.reshape(row_blocks, side, width)
    back_products = block_terms(values, row_ids, grad_source, live_count, True)
    partial_cols = jax.ops.segment_sum(back_products, col_ids, num_segments=col_blocks)
    own_cols = lax.psum_scatter(
        partial_cols.reshape(col_blocks * side, width), "row", scatter_dimension=0, tiled=True
    )
    grad_features = own_cols.astype(jnp.bfloat16).reshape(1, rows_here, width)
    return (activated, grad_weight, grad_features)


def densify_kernel(cb, rows_ref, cols_ref, count_ref, vals_ref, out_ref, acc):
    step = pl.program_id(0)
    chunk, side = vals_ref.shape[0], vals_ref.shape[1]
    cells = acc.shape[0]

    @pl.when(step == 0)
    def _():
        def zero(i, carry):
            acc[i] = jnp.zeros((side, side), F32)
            return carry

        lax.fori_loop(0, cells, zero, 0)

    first = step * chunk
    live = jnp.clip(count_ref[0] - first, 0, chunk)

    def add(i, carry):
        slot = first + i
        cell = rows_ref[slot] * cb + cols_ref[slot]
        acc[cell] = acc[cell] + vals_ref[i].astype(F32)
        return carry

    lax.fori_loop(0, live, add, 0)

    @pl.when(step == pl.num_programs(0) - 1)
    def _():
        def put(i, carry):
            for j in range(cb):
                out_ref[pl.ds(pl.multiple_of(i * side, side), side), j * side : (j + 1) * side] = acc[
                    i * cb + j
                ].astype(BF16)
            return carry

        lax.fori_loop(0, cells // cb, put, 0)


def densify(values, row_ids, col_ids, count, rb, cb):
    slots, side = values.shape[0], values.shape[1]
    chunk = 32
    return pl.pallas_call(
        functools.partial(densify_kernel, cb),
        out_shape=jax.ShapeDtypeStruct((rb * side, cb * side), BF16),
        grid_spec=pltpu.PrefetchScalarGridSpec(
            num_scalar_prefetch=3,
            grid=(slots // chunk,),
            in_specs=[pl.BlockSpec((chunk, side, side), lambda i, *_: (i, 0, 0))],
            out_specs=pl.BlockSpec((rb * side, cb * side), lambda i, *_: (0, 0)),
            scratch_shapes=[pltpu.VMEM((rb * cb, side, side), F32)],
        ),
        cost_estimate=pl.CostEstimate(
            flops=4 * values.size, bytes_accessed=2 * values.size + 2 * rb * cb * side * side, transcendentals=0
        ),
        name="densify",
    )(row_ids, col_ids, count, values)


def layer_kernel(nr, nc, *refs):
    x_refs = refs[:nr]
    (
        w_ref, ct_ref, a_hbm, act_ref, gw_ref, gf_ref,
        a_ref, xs, pf, sib_out, sib_in, chip_out, chip_in, gbuf, qt, z_out, z_in,
        lw, gw_in, gw_own, gw_row, gw_all,
        a_sem, x_sem, sib_s, sib_r, chip_s, chip_r, g_s, g_r, f_s, f_r, z_s, z_r,
        w1_s, w1_r, w2_s, w2_r, w3_s, w3_r,
    ) = refs[nr:]
    r = lax.axis_index("row")
    c = lax.axis_index("col")
    nq = nc // 2
    q = c // 2
    core = c % 2
    sib = 2 * q + (1 - core)
    rd, width = ct_ref.shape
    wr = width // nc

    def remote(src, dst, s, t, where):
        return pltpu.make_async_remote_copy(
            src_ref=src, dst_ref=dst, send_sem=s, recv_sem=t, device_id=where, device_id_type=MESH
        )

    def rows(i):
        return pl.ds(pl.multiple_of(i * rd, rd), rd)

    x_loads = [
        pltpu.make_async_copy(x, xs.at[rows((r + nr - j) % nr), :], x_sem.at[j]) for j, x in enumerate(x_refs)
    ]
    for load in x_loads:
        load.start()
    a_loads = []
    for i in range(nc):
        d = 2 * ((q + i % nq + 1) % nq) + (1 - core if i < nq else core)
        a_loads.append(pltpu.make_async_copy(a_hbm.at[rows(d), :], a_ref.at[rows(d), :], a_sem.at[i]))
    for load in a_loads:
        load.start()

    barrier = pltpu.get_barrier_semaphore()
    for j in range(1, nr):
        pl.semaphore_signal(barrier, inc=1, device_id={"row": (r + j) % nr}, device_id_type=MESH)
    for j in range(1, nc):
        pl.semaphore_signal(barrier, inc=1, device_id={"col": (c + j) % nc}, device_id_type=MESH)
    pl.semaphore_wait(barrier, nr + nc - 2)

    for load in x_loads:
        load.wait()

    def total(i, d):
        a_loads[i].wait()
        return jnp.dot(a_ref[rows(d), :], xs[...], preferred_element_type=F32)

    sib_copies = []
    for t in range(nq):
        chip = (q + t + 1) % nq
        sib_out[t] = total(t, 2 * chip + (1 - core)).astype(BF16)
        copy = remote(sib_out.at[t], sib_in.at[t], sib_s.at[t], sib_r.at[t], {"col": sib})
        copy.start()
        sib_copies.append(copy)
    chip_copies = []
    for t in range(nq):
        d = 2 * ((q + t + 1) % nq) + core
        value = total(nq + t, d)
        sib_copies[t].wait_recv()
        value = value + sib_in[t].astype(F32)
        if t < nq - 1:
            chip_out[t] = value.astype(BF16)
            copy = remote(chip_out.at[t], chip_in.at[t], chip_s.at[t], chip_r.at[t], {"col": d})
            copy.start()
            chip_copies.append(copy)
        else:
            pf[...] = value
    agg = pf[...]
    for t in range(nq - 1):
        chip_copies[t].wait_recv()
        agg = agg + chip_in[t].astype(F32)
    agg = agg.astype(BF16)

    pre = jnp.dot(agg, w_ref[...], preferred_element_type=F32)
    sigma = jax.nn.sigmoid(pre)
    act_ref[...] = (pre * sigma).astype(BF16)
    grad_pre = (ct_ref[...].astype(F32) * sigma * (1.0 + pre * (1.0 - sigma))).astype(BF16)
    gbuf[0, 0] = lax.dot_general(
        w_ref[...], grad_pre, (((1,), (1,)), ((), ())), preferred_element_type=F32
    ).astype(BF16)

    g_copies = [
        remote(gbuf.at[0, 0], gbuf.at[j, 0], g_s.at[j - 1], g_r.at[j - 1], {"col": 2 * ((q + j) % nq) + core})
        for j in range(1, nq)
    ]
    f_copies = [
        remote(gbuf.at[j, 0], gbuf.at[j, 1], f_s.at[j], f_r.at[j], {"col": sib}) for j in range(nq)
    ]
    for copy in g_copies:
        copy.start()
    f_copies[0].start()

    lw[...] = lax.dot_general(agg, grad_pre, (((0,), (0,)), ((), ())), preferred_element_type=F32)
    w1 = []
    for j in range(1, nc):
        d = (c + j) % nc
        copy = remote(
            lw.at[pl.ds(pl.multiple_of(d * wr, wr), wr), :], gw_in.at[j - 1],
            w1_s.at[j - 1], w1_r.at[j - 1], {"col": d},
        )
        copy.start()
        w1.append(copy)

    def a_rows(j, e):
        return rows(2 * ((q + nq - j) % nq) + (core if e == 0 else 1 - core))

    qt[...] = jnp.dot(gbuf[0, 0], a_ref[a_rows(0, 0), :], preferred_element_type=F32)
    for j in range(1, nq):
        f_copies[j - 1].wait_recv()
        qt[...] += jnp.dot(gbuf[j - 1, 1], a_ref[a_rows(j - 1, 1), :], preferred_element_type=F32)
        g_copies[j - 1].wait_recv()
        f_copies[j].start()
        qt[...] += jnp.dot(gbuf[j, 0], a_ref[a_rows(j, 0), :], preferred_element_type=F32)

    own_gw = lw[pl.ds(pl.multiple_of(c * wr, wr), wr), :]
    for copy in w1:
        copy.wait_recv()
    for j in range(1, nc):
        own_gw = own_gw + gw_in[j - 1]
    gw_own[...] = own_gw
    w2 = []
    for j in range(1, nr):
        copy = remote(gw_own, gw_row.at[j - 1], w2_s.at[j - 1], w2_r.at[j - 1], {"row": (r + j) % nr})
        copy.start()
        w2.append(copy)

    f_copies[nq - 1].wait_recv()
    z_copies = []
    for j in range(1, nr + 1):
        k = (r + j) % nr
        cols = rows(k)
        part = qt[:, cols] + jnp.dot(
            gbuf[nq - 1, 1], a_ref[a_rows(nq - 1, 1), cols], preferred_element_type=F32
        )
        if j < nr:
            z_out[j - 1] = part.astype(BF16)
            copy = remote(z_out.at[j - 1], z_in.at[j - 1], z_s.at[j - 1], z_r.at[j - 1], {"row": k})
            copy.start()
            z_copies.append(copy)
        else:
            pf[...] = part

    for copy in w2:
        copy.wait_recv()
    term = lambda i: jnp.where(
        i == r, own_gw, gw_row[jnp.maximum((r + nr - i) % nr, 1) - 1]
    )
    full = term(0)
    for i in range(1, nr):
        full = full + term(i)
    mine = pl.ds(pl.multiple_of(c * wr, wr), wr)
    gw_all[mine, :] = full
    w3 = []
    for j in range(1, nc):
        copy = remote(
            gw_all.at[mine, :], gw_all.at[mine, :], w3_s.at[j - 1], w3_r.at[j - 1], {"col": (c + j) % nc}
        )
        copy.start()
        w3.append(copy)

    grad = pf[...]
    for j in range(1, nr):
        z_copies[j - 1].wait_recv()
        grad = grad + z_in[j - 1].astype(F32)
    gf_ref[...] = grad.astype(BF16)
    for copy in w3:
        copy.wait_recv()
    gw_ref[...] = gw_all[...]
    for copy in sib_copies + chip_copies + g_copies + f_copies + w1 + w2 + z_copies + w3:
        copy.wait_send()


def tail_kernel(act_in, gw_in, gf_in, act_ref, gw_ref, gf_ref):
    act_ref[...] = act_in[...]
    gw_ref[...] = gw_in[...]
    gf_ref[...] = jnp.transpose(gf_in[...].astype(F32)).astype(BF16)


def dense_device(features, weight, cotangent, blk_vals, blk_rows, blk_cols, blk_count):
    nr, nc = lax.axis_size("row"), lax.axis_size("col")
    nq = nc // 2
    rd, width = cotangent.shape
    side = blk_vals.shape[-1]
    rb, cb = rd * nc // side, rd * nr // side
    held = [features[0]]
    for j in range(1, nr):
        held.append(lax.ppermute(features[0], "row", [(i, (i + j) % nr) for i in range(nr)]))
    panel = densify(blk_vals[0, 0], blk_rows[0, 0], blk_cols[0, 0], blk_count[0], rb, cb)
    vmem = pl.BlockSpec(memory_space=pltpu.VMEM)
    hbm = pl.BlockSpec(memory_space=pl.ANY)
    dma = pltpu.SemaphoreType.DMA
    wr = width // nc
    activated, grad_weight, grad_features = pl.pallas_call(
        functools.partial(layer_kernel, nr, nc),
        out_shape=(
            jax.ShapeDtypeStruct((rd, width), BF16),
            jax.ShapeDtypeStruct((width, width), F32),
            jax.ShapeDtypeStruct((width, rd), BF16),
        ),
        in_specs=[vmem] * (nr + 2) + [hbm],
        out_specs=(vmem, vmem, vmem),
        scratch_shapes=[
            pltpu.VMEM((rd * nc, rd * nr), BF16),
            pltpu.VMEM((rd * nr, width), BF16),
            pltpu.VMEM((rd, width), F32),
            pltpu.VMEM((nq, rd, width), BF16),
            pltpu.VMEM((nq, rd, width), BF16),
            pltpu.VMEM((nq - 1, rd, width), BF16),
            pltpu.VMEM((nq - 1, rd, width), BF16),
            pltpu.VMEM((nq, 2, width, rd), BF16),
            pltpu.VMEM((width, rd * nr), F32),
            pltpu.VMEM((nr - 1, width, rd), BF16),
            pltpu.VMEM((nr - 1, width, rd), BF16),
            pltpu.VMEM((width, width), F32),
            pltpu.VMEM((nc - 1, wr, width), F32),
            pltpu.VMEM((wr, width), F32),
            pltpu.VMEM((nr - 1, wr, width), F32),
            pltpu.VMEM((width, width), F32),
            dma((nc,)), dma((nr,)),
            dma((nq,)), dma((nq,)),
            dma((nq - 1,)), dma((nq - 1,)),
            dma((nq - 1,)), dma((nq - 1,)),
            dma((nq,)), dma((nq,)),
            dma((nr - 1,)), dma((nr - 1,)),
            dma((nc - 1,)), dma((nc - 1,)),
            dma((nr - 1,)), dma((nr - 1,)),
            dma((nc - 1,)), dma((nc - 1,)),
        ],
        compiler_params=pltpu.CompilerParams(collective_id=0, has_side_effects=True),
        name="layer",
    )(*held, weight, cotangent, panel)
    activated, grad_weight, grad_features = pl.pallas_call(
        tail_kernel,
        out_shape=(
            jax.ShapeDtypeStruct((rd, width), BF16),
            jax.ShapeDtypeStruct((width, width), F32),
            jax.ShapeDtypeStruct((rd, width), BF16),
        ),
        in_specs=[vmem] * 3,
        out_specs=(vmem, vmem, vmem),
        name="tail",
    )(activated, grad_weight, grad_features)
    return activated, grad_weight, grad_features[None]


def per_device(*arrays):
    blk_vals, cotangent = arrays[3], arrays[2]
    rd = cotangent.shape[0]
    panel_bytes = rd * lax.axis_size("col") * rd * lax.axis_size("row") * 4
    if panel_bytes <= DENSE_LIMIT:
        return dense_device(*arrays)
    return blockwise_device(*arrays)


def solution(mesh):
    return jax.shard_map(
        per_device,
        mesh=mesh,
        in_specs=(
            P("col", "row", None),
            P(),
            P(("row", "col"), None),
            P("row", "col", None, None, None),
            P("row", "col", None),
            P("row", "col", None),
            P("row", "col"),
        ),
        out_specs=(P(("row", "col"), None), P(), P("col", "row", None)),
        check_vma=False,
    )
```

```python
import functools

import jax
import jax.numpy as jnp
from jax import lax
from jax.experimental import pallas as pl
from jax.experimental.pallas import tpu as pltpu
from jax.sharding import PartitionSpec as P

MESH = pl.DeviceIdType.MESH
F32 = jnp.float32
BF16 = jnp.bfloat16
PARTS = 2
VMEM_GRANT = 28 * 1024 * 1024
DENSE_LIMIT = 16 * 1024 * 1024


def block_terms(values, index, source, live_count, transpose):
    total_slots = values.shape[0]
    group = 64
    width = source.shape[-1]
    side = values.shape[-1]
    if transpose:
        form = "bji,bjf->bif"
    else:
        form = "bij,bjf->bif"

    def one_group(group_index, buffer):
        first = group_index * group
        block_vals = lax.dynamic_slice_in_dim(values, first, group, 0)
        block_ids = lax.dynamic_slice_in_dim(index, first, group, 0)
        picked = jnp.take(source, block_ids, axis=0)
        product = jnp.einsum(form, block_vals, picked, preferred_element_type=jnp.float32)
        alive = first + jnp.arange(group, dtype=jnp.int32) < live_count
        product = jnp.where(alive[:, None, None], product, 0.0)
        return lax.dynamic_update_slice_in_dim(buffer, product, first, 0)

    buffer = jnp.zeros((total_slots, side, width), jnp.float32)
    groups = total_slots // group
    return lax.fori_loop(0, groups, one_group, buffer)


def blockwise_device(features, weight, cotangent, blk_vals, blk_rows, blk_cols, blk_count):
    rows_here = cotangent.shape[0]
    width = cotangent.shape[1]
    side = blk_vals.shape[-1]
    row_blocks = rows_here * lax.axis_size("col") // side
    col_blocks = rows_here * lax.axis_size("row") // side
    values = blk_vals[0, 0]
    row_ids = blk_rows[0, 0]
    col_ids = blk_cols[0, 0]
    live_count = blk_count[0, 0]
    panel = lax.all_gather(features, "row", axis=1, tiled=True)
    source = panel.reshape(col_blocks, side, width)
    products = block_terms(values, col_ids, source, live_count, False)
    partial_rows = jax.ops.segment_sum(products, row_ids, num_segments=row_blocks)
    own_rows = lax.psum_scatter(
        partial_rows.reshape(row_blocks * side, width), "col", scatter_dimension=0, tiled=True
    )
    aggregated = own_rows.astype(jnp.bfloat16)
    pre = jnp.dot(aggregated, weight, preferred_element_type=jnp.float32)
    sigma = jax.nn.sigmoid(pre)
    activated = (pre * sigma).astype(jnp.bfloat16)
    grad_pre = (cotangent.astype(jnp.float32) * sigma * (1.0 + pre * (1.0 - sigma))).astype(
        jnp.bfloat16
    )
    local_weight = lax.dot_general(
        aggregated, grad_pre, (((0,), (0,)), ((), ())), preferred_element_type=jnp.float32
    )
    grad_weight = lax.psum(local_weight, ("row", "col"))
    grad_agg = lax.dot_general(
        grad_pre, weight, (((1,), (1,)), ((), ())), preferred_element_type=jnp.float32
    ).astype(jnp.bfloat16)
    grad_rows = lax.all_gather(grad_agg, "col", axis=0, tiled=True)
    grad_source = grad_rows.reshape(row_blocks, side, width)
    back_products = block_terms(values, row_ids, grad_source, live_count, True)
    partial_cols = jax.ops.segment_sum(back_products, col_ids, num_segments=col_blocks)
    own_cols = lax.psum_scatter(
        partial_cols.reshape(col_blocks * side, width), "row", scatter_dimension=0, tiled=True
    )
    grad_features = own_cols.astype(jnp.bfloat16).reshape(1, rows_here, width)
    return (activated, grad_weight, grad_features)


def densify_kernel(cb, rows_ref, cols_ref, count_ref, vals, out_ref, acc):
    side = vals.shape[1]
    cells = acc.shape[0]

    def zero(i, carry):
        acc[i] = jnp.zeros((side, side), F32)
        return carry

    lax.fori_loop(0, cells, zero, 0)
    live = count_ref[0]

    def add(slot, carry):
        cell = rows_ref[slot] * cb + cols_ref[slot]
        acc[cell] = acc[cell] + vals[slot].astype(F32)
        return carry

    lax.fori_loop(0, live, add, 0)

    def put(i, carry):
        for j in range(cb):
            out_ref[pl.ds(pl.multiple_of(i * side, side), side), j * side : (j + 1) * side] = acc[
                i * cb + j
            ].astype(BF16)
        return carry

    lax.fori_loop(0, cells // cb, put, 0)


def densify(values, row_ids, col_ids, count, rb, cb):
    slots, side = values.shape[0], values.shape[1]
    smem = pl.BlockSpec(memory_space=pltpu.SMEM)
    return pl.pallas_call(
        functools.partial(densify_kernel, cb),
        out_shape=jax.ShapeDtypeStruct((rb * side, cb * side), BF16),
        in_specs=[smem, smem, smem, pl.BlockSpec(memory_space=pltpu.VMEM)],
        out_specs=pl.BlockSpec(memory_space=pltpu.VMEM),
        scratch_shapes=[
            pltpu.VMEM((rb * cb, side, side), F32),
        ],
        compiler_params=pltpu.CompilerParams(vmem_limit_bytes=VMEM_GRANT),
        cost_estimate=pl.CostEstimate(
            flops=4 * values.size, bytes_accessed=2 * values.size + 2 * rb * cb * side * side, transcendentals=0
        ),
        name="densify",
    )(row_ids, col_ids, count, values)


def layer_kernel(nr, nc, *refs):
    x_refs = refs[:nr]
    (
        w_ref, ct_ref, a_ref, act_ref, gw_ref, gf_ref,
        xs, pf, sib_out, sib_in, chip_out, chip_in, gbuf, qt, z_out, z_in,
        lw, gw_in, gw_own, gw_row, gw_all,
        x_sem, sib_s, sib_r, chip_s, chip_r, g_s, g_r, f_s, f_r, z_s, z_r,
        w1_s, w1_r, w2_s, w2_r, w3_s, w3_r,
    ) = refs[nr:]
    r = lax.axis_index("row")
    c = lax.axis_index("col")
    nq = nc // 2
    q = c // 2
    core = c % 2
    sib = 2 * q + (1 - core)
    rd, width = ct_ref.shape
    wr = width // nc
    pw = width // PARTS

    def remote(src, dst, s, t, where):
        return pltpu.make_async_remote_copy(
            src_ref=src, dst_ref=dst, send_sem=s, recv_sem=t, device_id=where, device_id_type=MESH
        )

    def rows(i):
        return pl.ds(pl.multiple_of(i * rd, rd), rd)

    x_loads = [
        pltpu.make_async_copy(x, xs.at[rows((r + nr - j) % nr), :], x_sem.at[j]) for j, x in enumerate(x_refs)
    ]
    for load in x_loads:
        load.start()
    barrier = pltpu.get_barrier_semaphore()
    for j in range(1, nr):
        pl.semaphore_signal(barrier, inc=1, device_id={"row": (r + j) % nr}, device_id_type=MESH)
    for j in range(1, nc):
        pl.semaphore_signal(barrier, inc=1, device_id={"col": (c + j) % nc}, device_id_type=MESH)
    pl.semaphore_wait(barrier, nr + nc - 2)

    for load in x_loads:
        load.wait()

    def total(d):
        return jnp.dot(a_ref[rows(d), :], xs[...], preferred_element_type=F32)

    sib_copies, chip_copies = [], []

    def give(t):
        sib_out[t] = total(2 * ((q + t + 1) % nq) + (1 - core)).astype(BF16)
        copy = remote(sib_out.at[t], sib_in.at[t], sib_s.at[t], sib_r.at[t], {"col": sib})
        copy.start()
        sib_copies.append(copy)

    give(0)
    for t in range(nq):
        if t < nq - 1:
            give(t + 1)
        d = 2 * ((q + t + 1) % nq) + core
        value = total(d)
        sib_copies[t].wait_recv()
        value = value + sib_in[t].astype(F32)
        if t < nq - 1:
            chip_out[t] = value.astype(BF16)
            copy = remote(chip_out.at[t], chip_in.at[t], chip_s.at[t], chip_r.at[t], {"col": d})
            copy.start()
            chip_copies.append(copy)
        else:
            pf[...] = value
    agg = pf[...]
    for t in range(nq - 1):
        chip_copies[t].wait_recv()
        agg = agg + chip_in[t].astype(F32)
    agg = agg.astype(BF16)

    pre = jnp.dot(agg, w_ref[...], preferred_element_type=F32)
    sigma = jax.nn.sigmoid(pre)
    act_ref[...] = (pre * sigma).astype(BF16)
    grad_pre = (ct_ref[...].astype(F32) * sigma * (1.0 + pre * (1.0 - sigma))).astype(BF16)
    def part(h):
        return pl.ds(h * pw, pw)

    def at(j, h):
        return j * PARTS + h

    local = lax.dot_general(agg, grad_pre, (((0,), (0,)), ((), ())), preferred_element_type=F32)
    lw[...] = local.astype(BF16)
    gw_all[...] = local
    mine = pl.ds(pl.multiple_of(c * wr, wr), wr)
    w1 = []
    for j in range(1, nc):
        d = (c + j) % nc
        copy = remote(
            lw.at[pl.ds(pl.multiple_of(d * wr, wr), wr), :], gw_in.at[j - 1],
            w1_s.at[j - 1], w1_r.at[j - 1], {"col": d},
        )
        copy.start()
        w1.append(copy)
    g_copies, f_copies = {}, {}
    for h in range(PARTS):
        gbuf[0, 0, part(h), :] = lax.dot_general(
            w_ref[part(h), :], grad_pre, (((1,), (1,)), ((), ())), preferred_element_type=F32
        ).astype(BF16)
        for j in range(1, nq):
            g_copies[j, h] = remote(
                gbuf.at[0, 0, part(h), :], gbuf.at[j, 0, part(h), :],
                g_s.at[at(j - 1, h)], g_r.at[at(j - 1, h)], {"col": 2 * ((q + j) % nq) + core},
            )
            g_copies[j, h].start()
        for j in range(nq):
            f_copies[j, h] = remote(
                gbuf.at[j, 0, part(h), :], gbuf.at[j, 1, part(h), :],
                f_s.at[at(j, h)], f_r.at[at(j, h)], {"col": sib},
            )
        f_copies[0, h].start()

    own_gw = gw_all[mine, :]

    def a_rows(j, e):
        return rows(2 * ((q + nq - j) % nq) + (core if e == 0 else 1 - core))

    def product(j, e, h):
        return jnp.dot(gbuf[j, e, part(h), :], a_ref[a_rows(j, e), :], preferred_element_type=F32)

    z_copies = {}
    w2 = []
    for h in range(PARTS):
        qt[...] = product(0, 0, h)
        for j in range(1, nq):
            f_copies[j - 1, h].wait_recv()
            qt[...] += product(j - 1, 1, h)
            g_copies[j, h].wait_recv()
            f_copies[j, h].start()
            qt[...] += product(j, 0, h)
        if h == 0:
            for copy in w1:
                copy.wait_recv()
            for j in range(1, nc):
                own_gw = own_gw + gw_in[j - 1].astype(F32)
            gw_own[...] = own_gw.astype(BF16)
            for j in range(1, nr):
                copy = remote(
                    gw_own, gw_row.at[j - 1], w2_s.at[j - 1], w2_r.at[j - 1], {"row": (r + j) % nr}
                )
                copy.start()
                w2.append(copy)
        f_copies[nq - 1, h].wait_recv()
        for j in range(1, nr + 1):
            k = (r + j) % nr
            cols = rows(k)
            value = qt[:, cols] + jnp.dot(
                gbuf[nq - 1, 1, part(h), :], a_ref[a_rows(nq - 1, 1), cols], preferred_element_type=F32
            )
            if j < nr:
                z_out[j - 1, part(h), :] = value.astype(BF16)
                z_copies[j, h] = remote(
                    z_out.at[j - 1, part(h), :], z_in.at[j - 1, part(h), :],
                    z_s.at[at(j - 1, h)], z_r.at[at(j - 1, h)], {"row": k},
                )
                z_copies[j, h].start()
            else:
                pf[part(h), :] = value
    own_gw = gw_own[...].astype(F32)

    for copy in w2:
        copy.wait_recv()
    term = lambda i: jnp.where(
        i == r, own_gw, gw_row[jnp.maximum((r + nr - i) % nr, 1) - 1].astype(F32)
    )
    full = term(0)
    for i in range(1, nr):
        full = full + term(i)
    gw_all[mine, :] = full
    w3 = []
    for j in range(1, nc):
        copy = remote(
            gw_all.at[mine, :], gw_all.at[mine, :], w3_s.at[j - 1], w3_r.at[j - 1], {"col": (c + j) % nc}
        )
        copy.start()
        w3.append(copy)

    for h in range(PARTS):
        grad = pf[part(h), :]
        for j in range(1, nr):
            z_copies[j, h].wait_recv()
            grad = grad + z_in[j - 1, part(h), :].astype(F32)
        gf_ref[part(h), :] = grad.astype(BF16)
    for copy in w3:
        copy.wait_recv()
    gw_ref[...] = gw_all[...]
    for copy in sib_copies + chip_copies + w1 + w2 + w3:
        copy.wait_send()
    for copies in (g_copies, f_copies, z_copies):
        for copy in copies.values():
            copy.wait_send()


def tail_kernel(act_in, gw_in, gf_in, act_ref, gw_ref, gf_ref):
    act_ref[...] = act_in[...]
    gw_ref[...] = gw_in[...]
    gf_ref[...] = jnp.transpose(gf_in[...].astype(F32)).astype(BF16)


def dense_device(features, weight, cotangent, blk_vals, blk_rows, blk_cols, blk_count):
    nr, nc = lax.axis_size("row"), lax.axis_size("col")
    nq = nc // 2
    rd, width = cotangent.shape
    side = blk_vals.shape[-1]
    rb, cb = rd * nc // side, rd * nr // side
    held = [features[0]]
    for j in range(1, nr):
        held.append(lax.ppermute(features[0], "row", [(i, (i + j) % nr) for i in range(nr)]))
    panel = densify(blk_vals[0, 0], blk_rows[0, 0], blk_cols[0, 0], blk_count[0], rb, cb)
    vmem = pl.BlockSpec(memory_space=pltpu.VMEM)
    dma = pltpu.SemaphoreType.DMA
    wr = width // nc
    activated, grad_weight, grad_features = pl.pallas_call(
        functools.partial(layer_kernel, nr, nc),
        out_shape=(
            jax.ShapeDtypeStruct((rd, width), BF16),
            jax.ShapeDtypeStruct((width, width), F32),
            jax.ShapeDtypeStruct((width, rd), BF16),
        ),
        in_specs=[vmem] * (nr + 3),
        out_specs=(vmem, vmem, vmem),
        scratch_shapes=[
            pltpu.VMEM((rd * nr, width), BF16),
            pltpu.VMEM((rd, width), F32),
            pltpu.VMEM((nq, rd, width), BF16),
            pltpu.VMEM((nq, rd, width), BF16),
            pltpu.VMEM((nq - 1, rd, width), BF16),
            pltpu.VMEM((nq - 1, rd, width), BF16),
            pltpu.VMEM((nq, 2, width, rd), BF16),
            pltpu.VMEM((width // PARTS, rd * nr), F32),
            pltpu.VMEM((nr - 1, width, rd), BF16),
            pltpu.VMEM((nr - 1, width, rd), BF16),
            pltpu.VMEM((width, width), BF16),
            pltpu.VMEM((nc - 1, wr, width), BF16),
            pltpu.VMEM((wr, width), BF16),
            pltpu.VMEM((nr - 1, wr, width), BF16),
            pltpu.VMEM((width, width), F32),
            dma((nr,)),
            dma((nq,)), dma((nq,)),
            dma((nq - 1,)), dma((nq - 1,)),
            dma(((nq - 1) * PARTS,)), dma(((nq - 1) * PARTS,)),
            dma((nq * PARTS,)), dma((nq * PARTS,)),
            dma(((nr - 1) * PARTS,)), dma(((nr - 1) * PARTS,)),
            dma((nc - 1,)), dma((nc - 1,)),
            dma((nr - 1,)), dma((nr - 1,)),
            dma((nc - 1,)), dma((nc - 1,)),
        ],
        compiler_params=pltpu.CompilerParams(collective_id=0, has_side_effects=True, vmem_limit_bytes=VMEM_GRANT),
        name="layer",
    )(*held, weight, cotangent, panel)
    activated, grad_weight, grad_features = pl.pallas_call(
        tail_kernel,
        out_shape=(
            jax.ShapeDtypeStruct((rd, width), BF16),
            jax.ShapeDtypeStruct((width, width), F32),
            jax.ShapeDtypeStruct((rd, width), BF16),
        ),
        in_specs=[vmem] * 3,
        out_specs=(vmem, vmem, vmem),
        compiler_params=pltpu.CompilerParams(vmem_limit_bytes=VMEM_GRANT),
        name="tail",
    )(activated, grad_weight, grad_features)
    return activated, grad_weight, grad_features[None]


def per_device(*arrays):
    blk_vals, cotangent = arrays[3], arrays[2]
    rd = cotangent.shape[0]
    panel_bytes = rd * lax.axis_size("col") * rd * lax.axis_size("row") * 4
    if panel_bytes <= DENSE_LIMIT:
        return dense_device(*arrays)
    return blockwise_device(*arrays)


def solution(mesh):
    return jax.shard_map(
        per_device,
        mesh=mesh,
        in_specs=(
            P("col", "row", None),
            P(),
            P(("row", "col"), None),
            P("row", "col", None, None, None),
            P("row", "col", None),
            P("row", "col", None),
            P("row", "col"),
        ),
        out_specs=(P(("row", "col"), None), P(), P("col", "row", None)),
        check_vma=False,
    )
```
